256 devices in a mesh: ctx: 8 (over z), head: 32 (over y, x, core).
Axes of the slice: x: 4, y: 4, z: 8, core: 2. Of those that a mesh axis runs over, the one named last changes fastest.
Arguments:
- hidden: float32 [2048, 2304], P(('ctx', 'head')), may hold values from -40 to 40
- w_query: float32 [2304, 6144], P(None, 'head'), may hold values from -0.125 to 0.125
- w_down: float32 [2304, 576], replicated, may hold values from -0.125 to 0.125
- latent_gain: float32 [512], replicated, may hold values from 0.25 to 1.75
- w_key_up: float32 [512, 4096], P(None, 'head'), may hold values from -0.25 to 0.25
- w_value_up: float32 [512, 4096], P(None, 'head'), may hold values from -0.25 to 0.25
- w_out: float32 [4096, 2304], P('head'), may hold values from -0.09375 to 0.09375
Outputs:
- output: float32 [2048, 2304], P(('ctx', 'head'))
The draws below stay inside these ranges and needn't reach their ends.
All inputs are finite; a program needn't handle non-finite values.
Results may differ from the reference program's by a relative error of at most 0.0003.
Values sent between devices are 32-bit elements; how exact they have to be, the bound alone decides.
No kernel may reach another device: no remote copies, remote signals or barrier semaphores. Data moves between devices by JAX's collectives and lax.ppermute only.
A program may use at most 64 MiB of HBM per device.

```python
import jax
import jax.numpy as jnp
from jax import lax

D = 2304
HEADS = 32
RANK = 512
SHARED = 64
NOPE = 128
VDIM = 128
TOKENS = 2048


def draw_hidden(key, part):
    base_key = jax.random.fold_in(jax.random.fold_in(key, 17), 0)
    values = jnp.clip(jax.random.normal(base_key, (TOKENS, D), jnp.float32), -4.0, 4.0)
    return values.astype(jnp.float32)


def level_of(rng, extent, shards, low, largest):
    level = 1.0
    for position, parts in shards:
        steps = jax.random.uniform(jax.random.fold_in(jax.random.fold_in(rng, 6), position), (parts,), jnp.float32, low / len(shards), largest / len(shards))
        level = level * jnp.repeat(jnp.exp(steps), extent[position] // parts).reshape((-1,) + (1,) * (len(extent) - 1 - position))
    return level


def centred(stream_key, dims, width, reach, cuts=(), kind=jnp.bfloat16):
    array = jax.random.normal(stream_key, dims, jnp.float32) * width
    if len(cuts) > 0:
        array = level_of(stream_key, dims, cuts, -0.22, 0.18) * array
    return jnp.clip(array, min=-reach, max=reach).astype(kind)


def setup_inputs(seed: int = 0) -> dict:
    key_of = jax.random.split(jax.random.key(seed), 8)
    hidden = draw_hidden(jax.random.fold_in(key_of[7], 71), 0)
    w_query = centred(key_of[1], (D, HEADS * (NOPE + SHARED)), D ** -0.5, 0.125, ((1, 32),), jnp.float32)
    w_down = centred(key_of[2], (D, RANK + SHARED), D ** -0.5, 0.125, (), jnp.float32)
    latent_gain = jnp.clip(1.0 + 0.15 * jax.random.normal(key_of[3], (RANK,), jnp.float32), 0.25, 1.75)
    w_key_up = centred(key_of[4], (RANK, HEADS * NOPE), RANK ** -0.5, 0.25, ((1, 32),), jnp.float32)
    w_value_up = centred(key_of[5], (RANK, HEADS * VDIM), RANK ** -0.5, 0.25, ((1, 32),), jnp.float32)
    w_out = centred(key_of[6], (HEADS * VDIM, D), (HEADS * VDIM) ** -0.5, 0.09375, ((0, 32),), jnp.float32)
    return dict(hidden=hidden, w_query=w_query, w_down=w_down, latent_gain=latent_gain, w_key_up=w_key_up, w_value_up=w_value_up, w_out=w_out)


EXACT = lax.Precision.HIGHEST

def matmul(left, right):
    return jnp.dot(left, right, precision=EXACT, preferred_element_type=jnp.float32)

def reference(hidden, w_query, w_down, latent_gain, w_key_up, w_value_up, w_out):
    down_part = matmul(hidden, w_down)
    raw_latent = down_part[:, :RANK]
    key_shared = down_part[:, RANK:]
    meansq = lax.optimization_barrier(jnp.mean(raw_latent * raw_latent, axis=-1, keepdims=True))
    latent = raw_latent * lax.rsqrt(meansq + 1e-06) * latent_gain
    queries = matmul(hidden, w_query).reshape(TOKENS, HEADS, NOPE + SHARED).transpose(1, 0, 2)
    key_own = matmul(latent, w_key_up).reshape(TOKENS, HEADS, NOPE).transpose(1, 0, 2)
    values = matmul(latent, w_value_up).reshape(TOKENS, HEADS, VDIM).transpose(1, 0, 2)
    positions = jnp.arange(TOKENS, dtype=jnp.int32)
    causal = positions[:, None] >= positions[None, :]
    score_scale = (NOPE + SHARED) ** (-0.5)

    def per_head(operands):
        head_query, head_key, head_value = operands
        scores = (matmul(head_query[:, :NOPE], head_key.T) + matmul(head_query[:, NOPE:], key_shared.T)) * score_scale
        scores = jnp.where(causal, scores, -jnp.inf)
        weights = jax.nn.softmax(scores, axis=-1)
        return matmul(weights, head_value)
    attended = lax.map(per_head, (queries, key_own, values))
    attended = attended.transpose(1, 0, 2).reshape(TOKENS, HEADS * VDIM)
    return matmul(attended, w_out)
```

```python
import jax
import jax.numpy as jnp
from jax import lax
from jax.sharding import PartitionSpec as P

EXACT = lax.Precision.HIGHEST
EPSILON = 1e-06
FLOOR = -1e30
RING = (1, -1, 2, -2)
FAR = (3, 4, 5)


def matmul(left, right):
    return jnp.dot(left, right, precision=EXACT, preferred_element_type=jnp.float32)


def partner(array):
    size = lax.axis_size("head")
    return lax.ppermute(array, "head", [(h, h ^ 1) for h in range(size)])


def from_behind(array, step):
    size = lax.axis_size("ctx")
    return lax.ppermute(array, "ctx", [(c, (c + step) % size) for c in range(size)])


def exchange(pieces):
    size = lax.axis_size("head")
    groups = [list(range(core, size, 2)) for core in range(2)]
    return lax.all_to_all(
        pieces, "head", split_axis=0, concat_axis=0, tiled=True, axis_index_groups=groups
    )


def spread(array):
    count = lax.axis_size("head") // 2
    copies = jnp.broadcast_to(array[None], (count, *array.shape))
    return exchange(copies)


def partial_attention(queries, latent, weights, q_pos, k_pos, scale):
    rank = weights[0][0].shape[0]
    causal = q_pos[:, None] >= k_pos[None, :]
    key_shared = latent[:, rank:]
    pieces = []
    for query, (key_up, value_up) in zip(queries, weights):
        nope = key_up.shape[1]
        key = jnp.concatenate([matmul(latent[:, :rank], key_up), key_shared], axis=1)
        value = matmul(latent[:, :rank], value_up)
        scores = jnp.where(causal, matmul(query, key.T) * scale, FLOOR)
        top = jnp.max(scores, axis=1, keepdims=True)
        weight = jnp.where(causal, jnp.exp(scores - top), 0.0)
        pieces.append((top, jnp.sum(weight, axis=1, keepdims=True), matmul(weight, value)))
    return pieces


def merged(parts):
    top = parts[0][0]
    for part in parts[1:]:
        top = jnp.maximum(top, part[0])
    total = sum(part[1] * jnp.exp(part[0] - top) for part in parts)
    acc = sum(part[2] * jnp.exp(part[0] - top) for part in parts)
    return top, total, acc


def on_device(hidden, w_query, w_down, latent_gain, w_key_up, w_value_up, w_out):
    rank = w_key_up.shape[0]
    rows = hidden.shape[0]
    blocks = lax.axis_size("ctx")
    ctx = lax.axis_index("ctx")
    head = lax.axis_index("head")
    core, place = head % 2, head // 2
    places = lax.axis_size("head") // 2
    block_rows = 2 * places * rows
    scale = w_query.shape[1] ** (-0.5)

    far_query, far_key, far_value, far_out = (
        partner(w_query),
        partner(w_key_up),
        partner(w_value_up),
        partner(w_out),
    )
    mine = spread(hidden).reshape(places * rows, hidden.shape[1])

    down = matmul(mine, w_down)
    raw = down[:, :rank]
    meansq = jnp.mean(raw * raw, axis=-1, keepdims=True)
    latent = jnp.concatenate(
        [raw * lax.rsqrt(meansq + EPSILON) * latent_gain, down[:, rank:]], axis=1
    )
    own_rows = lax.dynamic_slice(latent, (place * rows, 0), (rows, latent.shape[1]))

    far = [from_behind(own_rows, step) for step in FAR]
    ring = [from_behind(latent, step) for step in RING]

    q_mine = matmul(mine, w_query)
    q_other = matmul(mine, far_query)
    arrived = partner(jnp.concatenate([q_mine, q_other], axis=1))
    width = w_query.shape[1]
    queries = [
        jnp.concatenate([q_mine, arrived[:, width:]], axis=0),
        jnp.concatenate([q_other, arrived[:, :width]], axis=0),
    ]
    weights = [(w_key_up, w_value_up), (far_key, far_value)]

    def offsets(place_of, row_of, cls):
        return (place_of * 2 + cls) * rows + row_of

    half = jnp.arange(places * rows, dtype=jnp.int32)
    mine_off = offsets(half // rows, half % rows, core)
    other_off = offsets(half // rows, half % rows, 1 - core)
    q_pos = ctx * block_rows + jnp.concatenate([mine_off, other_off])

    parts = [
        partial_attention(
            queries, latent, weights, q_pos, ctx * block_rows + mine_off, scale
        )
    ]
    ring_pos = jnp.concatenate(
        [((ctx - step) % blocks) * block_rows + mine_off for step in RING]
    )
    parts.append(
        partial_attention(
            queries, jnp.concatenate(ring, axis=0), weights, q_pos, ring_pos, scale
        )
    )
    far_latent = spread(jnp.stack(far)).reshape(-1, latent.shape[1])
    index = jnp.arange(far_latent.shape[0], dtype=jnp.int32)
    far_place = index // (len(FAR) * rows)
    far_step = FAR[0] + (index // rows) % len(FAR)
    far_pos = ((ctx - far_step) % blocks) * block_rows + offsets(far_place, index % rows, core)
    parts.append(partial_attention(queries, far_latent, weights, q_pos, far_pos, scale))

    own_count = places * rows
    kept, sent = [], []
    for number in range(2):
        top, total, acc = merged([part[number] for part in parts])
        stats = jnp.concatenate([acc, jnp.broadcast_to(top, acc.shape), jnp.broadcast_to(total, acc.shape)], axis=1)
        kept.append((top[:own_count], total[:own_count], acc[:own_count]))
        sent.append(stats[own_count:])
    arrived = partner(jnp.stack(sent[::-1]))
    vdim = w_value_up.shape[1]
    attended = []
    for number in range(2):
        piece = arrived[number]
        other = (piece[:, vdim : vdim + 1], piece[:, 2 * vdim : 2 * vdim + 1], piece[:, :vdim])
        top, total, acc = merged([kept[number], other])
        attended.append(acc / total)
    shares = matmul(attended[0], w_out) + matmul(attended[1], far_out)
    arrived = exchange(shares.reshape(places, rows, shares.shape[1]))
    return arrived.sum(axis=0)


def solution(mesh):
    placed = (
        P(("ctx", "head"), None),
        P(None, "head"),
        P(),
        P(),
        P(None, "head"),
        P(None, "head"),
        P("head", None),
    )
    return jax.shard_map(
        on_device, mesh=mesh, in_specs=placed, out_specs=P(("ctx", "head"), None), check_vma=False
    )
```

```python
import functools

import jax
import jax.numpy as jnp
from jax import lax
from jax.experimental import pallas as pl
from jax.experimental.pallas import tpu as pltpu
from jax.sharding import PartitionSpec as P

EXACT = lax.Precision.HIGHEST
EPSILON = 1e-06
FLOOR = -1e30
VMEM = pltpu.VMEM


def dot_nn(left, right):
    return lax.dot_general(
        left, right, (((1,), (0,)), ((), ())), precision=EXACT, preferred_element_type=jnp.float32
    )


def dot_nt(left, right):
    return lax.dot_general(
        left, right, (((1,), (1,)), ((), ())), precision=EXACT, preferred_element_type=jnp.float32
    )


def call(kernel, out_shape, *operands, name):
    return pl.pallas_call(
        kernel,
        out_shape=jax.ShapeDtypeStruct(out_shape, jnp.float32),
        in_specs=[pl.BlockSpec(memory_space=VMEM)] * len(operands),
        out_specs=pl.BlockSpec(memory_space=VMEM),
        compiler_params=pltpu.CompilerParams(vmem_limit_bytes=48 << 20),
        name=name,
    )(*operands)


def latent_kernel(x_ref, down_ref, gain_ref, out_ref):
    rank = gain_ref.shape[1]
    down = dot_nt(x_ref[...], down_ref[...])
    raw = down[:, :rank]
    meansq = jnp.mean(raw * raw, axis=-1, keepdims=True)
    out_ref[:, :rank] = raw * lax.rsqrt(meansq + EPSILON) * gain_ref[...]
    out_ref[:, rank:] = down[:, rank:]


def query_kernel(x_ref, own_ref, other_ref, out_ref):
    out_ref[0] = dot_nt(x_ref[...], own_ref[...])
    out_ref[1] = dot_nt(x_ref[...], other_ref[...])


def token_offset(index, cls, rows, half):
    within = lax.rem(index, half)
    return (within // rows * 2 + cls) * rows + lax.rem(within, rows)


def attend_kernel(rows, scale, blocks, pieces, fresh, place_ref, *refs):
    query_ref, key_ref, value_ref, far_key_ref, far_value_ref = refs[:5]
    latent_refs = refs[5 : 5 + len(pieces)]
    out_ref = refs[-1]
    ctx, core = place_ref[0], place_ref[1]
    rank = key_ref.shape[0]
    nope = key_ref.shape[1]
    vdim = value_ref.shape[1]
    count = query_ref.shape[1]
    half = count // 2
    latent = jnp.concatenate([ref[...] for ref in latent_refs], axis=0)
    keys = latent.shape[0]

    row = lax.broadcasted_iota(jnp.int32, (count, 1), 0)
    row_cls = jnp.where(row < half, core, 1 - core)
    q_pos = ctx * count + token_offset(row, row_cls, rows, half)
    column = lax.broadcasted_iota(jnp.int32, (1, keys), 1)
    block = jnp.zeros((1, keys), jnp.int32)
    start = 0
    for (step, first), ref in zip(pieces, latent_refs):
        source = lax.rem(ctx - step + blocks, blocks)
        inside = (column >= start) & (column < start + ref.shape[0])
        block = jnp.where(inside, source, block)
        start += ref.shape[0]
    k_pos = block * count + token_offset(column, core, rows, half)
    causal = q_pos >= k_pos

    compressed = latent[:, :rank]
    key_shared = latent[:, rank:]
    for head, (up_k, up_v) in enumerate(((key_ref, value_ref), (far_key_ref, far_value_ref))):
        key = dot_nn(compressed, up_k[...])
        value = dot_nn(compressed, up_v[...])
        query = query_ref[head]
        scores = (dot_nt(query[:, :nope], key) + dot_nt(query[:, nope:], key_shared)) * scale
        scores = jnp.where(causal, scores, FLOOR)
        top = jnp.max(scores, axis=1, keepdims=True)
        if not fresh:
            state_ref = refs[5 + len(pieces)]
            before = state_ref[head, :, vdim : vdim + 1]
            top = jnp.maximum(top, before)
        weight = jnp.where(causal, jnp.exp(scores - top), 0.0)
        total = jnp.sum(weight, axis=1, keepdims=True)
        acc = dot_nn(weight, value)
        if not fresh:
            fade = jnp.exp(before - top)
            total = total + state_ref[head, :, vdim + 64 : vdim + 65] * fade
            acc = acc + state_ref[head, :, :vdim] * fade
        out_ref[head, :, :vdim] = acc
        out_ref[head, :, vdim : vdim + 64] = jnp.broadcast_to(top, (count, 64))
        out_ref[head, :, vdim + 64 :] = jnp.broadcast_to(total, (count, 64))


def share_kernel(state_ref, arrived_ref, out_w_ref, far_out_ref, out_ref):
    vdim = out_w_ref.shape[0]
    half = arrived_ref.shape[1]
    attended = []
    for head in range(2):
        mine = state_ref[head, :half]
        other = arrived_ref[1 - head]
        m0, m1 = mine[:, vdim : vdim + 1], other[:, vdim : vdim + 1]
        top = jnp.maximum(m0, m1)
        f0, f1 = jnp.exp(m0 - top), jnp.exp(m1 - top)
        total = mine[:, vdim + 64 : vdim + 65] * f0 + other[:, vdim + 64 : vdim + 65] * f1
        attended.append((mine[:, :vdim] * f0 + other[:, :vdim] * f1) / total)
    out_ref[...] = dot_nn(attended[0], out_w_ref[...]) + dot_nn(attended[1], far_out_ref[...])


def partner(array):
    size = lax.axis_size("head")
    return lax.ppermute(array, "head", [(h, h ^ 1) for h in range(size)])


def from_behind(array, step):
    size = lax.axis_size("ctx")
    return lax.ppermute(array, "ctx", [(c, (c + step) % size) for c in range(size)])


def exchange(pieces):
    size = lax.axis_size("head")
    groups = [list(range(core, size, 2)) for core in range(2)]
    return lax.all_to_all(
        pieces, "head", split_axis=0, concat_axis=0, tiled=True, axis_index_groups=groups
    )


def on_device(hidden, w_query, w_down, latent_gain, w_key_up, w_value_up, w_out):
    rows = hidden.shape[0]
    blocks = lax.axis_size("ctx")
    places = lax.axis_size("head") // 2
    scale = w_query.shape[1] ** (-0.5)
    place = jnp.stack([lax.axis_index("ctx"), lax.axis_index("head") & 1]).astype(jnp.int32)

    copies = jnp.broadcast_to(hidden[None], (places, *hidden.shape))
    mine = exchange(copies).reshape(places * rows, hidden.shape[1])
    far_query = partner(w_query)
    far_key = partner(w_key_up)
    far_value = partner(w_value_up)
    far_out = partner(w_out)

    width = w_down.shape[1]
    latent = call(
        latent_kernel, (places * rows, width), mine, w_down.T, latent_gain[None], name="latent"
    )
    ring = {step: from_behind(latent, step) for step in (1, -1, 2, -2)}
    half = latent.shape[0] // 2

    q_mine = call(
        query_kernel,
        (2, places * rows, w_query.shape[1]),
        mine,
        w_query.T,
        far_query.T,
        name="query",
    )
    q_other = partner(q_mine)
    queries = jnp.concatenate([q_mine, q_other[::-1]], axis=1)

    def attend(pieces, latents, state):
        kernel = functools.partial(attend_kernel, rows, scale, blocks, pieces, state is None)
        operands = [queries, w_key_up, w_value_up, far_key, far_value, *latents]
        if state is not None:
            operands.append(state)
        return pl.pallas_call(
            kernel,
            out_shape=jax.ShapeDtypeStruct(
                (2, queries.shape[1], 2 * w_value_up.shape[1]), jnp.float32
            ),
            in_specs=[pl.BlockSpec(memory_space=pltpu.SMEM)]
            + [pl.BlockSpec(memory_space=VMEM)] * len(operands),
            out_specs=pl.BlockSpec(memory_space=VMEM),
            compiler_params=pltpu.CompilerParams(vmem_limit_bytes=48 << 20),
            name="attend",
        )(place, *operands)

    state = attend([(0, 0)], [latent], None)
    state = attend([(k, 0) for k in ring], list(ring.values()), state)
    relay = [
        from_behind(ring[2], 1),
        from_behind(ring[-2], -1),
        from_behind(ring[2][:half], 2),
        from_behind(ring[-2][half:], -2),
    ]
    state = attend([(3, 0), (-3, 0), (4, 0), (4, half)], relay, state)

    arrived = partner(state[:, places * rows :])
    shares = call(
        share_kernel,
        (places * rows, w_out.shape[1]),
        state,
        arrived,
        w_out,
        far_out,
        name="share",
    )
    return exchange(shares.reshape(places, rows, shares.shape[1])).sum(axis=0)


def solution(mesh):
    placed = (
        P(("ctx", "head"), None),
        P(None, "head"),
        P(),
        P(),
        P(None, "head"),
        P(None, "head"),
        P("head", None),
    )
    return jax.shard_map(
        on_device, mesh=mesh, in_specs=placed, out_specs=P(("ctx", "head"), None), check_vma=False
    )
```

```python
import functools

import jax
import jax.numpy as jnp
from jax import lax
from jax.experimental import pallas as pl
from jax.experimental.pallas import tpu as pltpu
from jax.sharding import PartitionSpec as P

EPSILON = 1e-06
FLOOR = -1e30
RING = (1, -1)
FAR = (2, 3, 4, 5, 6)
F32 = jnp.float32
BF16 = jnp.bfloat16
VMEM = pltpu.VMEM
LIMIT = 24 << 20


def nn(left, right):
    return lax.dot_general(left, right, (((1,), (0,)), ((), ())), preferred_element_type=F32)


def nt(left, right):
    return lax.dot_general(left, right, (((1,), (1,)), ((), ())), preferred_element_type=F32)


def split(array, count):
    parts = []
    for _ in range(count - 1):
        part = array.astype(BF16)
        parts.append(part)
        array = array - part.astype(F32)
    parts.append(array.astype(BF16))
    return parts


def six(left, right, dot):
    high, middle, low = left
    rows = high.shape[0]
    by_high = dot(jnp.concatenate([high, middle, low], axis=0), right[0])
    by_middle = dot(jnp.concatenate([high, middle], axis=0), right[1])
    by_low = dot(high, right[2])
    return by_high[:rows] + (
        (by_high[rows : 2 * rows] + by_middle[:rows])
        + (by_high[2 * rows :] + by_middle[rows:] + by_low)
    )


def three(left, right, dot):
    high, low = left[:2]
    rows = high.shape[0]
    by_high = dot(jnp.concatenate([high, low], axis=0), right[0])
    return by_high[:rows] + (by_high[rows:] + dot(high, right[1]))


def call(kernel, outs, operands, name, place=None):
    first = [] if place is None else [place]
    return pl.pallas_call(
        kernel,
        out_shape=outs,
        in_specs=[pl.BlockSpec(memory_space=pltpu.SMEM)] * len(first)
        + [pl.BlockSpec(memory_space=VMEM)] * len(operands),
        out_specs=jax.tree.map(lambda _: pl.BlockSpec(memory_space=VMEM), outs),
        compiler_params=pltpu.CompilerParams(vmem_limit_bytes=LIMIT),
        name=name,
    )(*first, *operands)


def shape(*dims, dtype=F32):
    return jax.ShapeDtypeStruct(dims, dtype)


def split_kernel(count, *refs):
    sources, outs = refs[:-1], refs[-1]
    start = 0
    for ref in sources:
        stop = start + ref.shape[0]
        for part, value in enumerate(split(ref[...], count)):
            outs[part, start:stop] = value
        start = stop


def normed(down, gain, out_ref):
    rank = gain.shape[1]
    raw = down[:, :rank]
    meansq = jnp.mean(raw * raw, axis=-1, keepdims=True)
    out_ref[:, :rank] = raw * lax.rsqrt(meansq + EPSILON) * gain
    out_ref[:, rank:] = down[:, rank:]


def own_kernel(x_ref, down_ref, gain_ref, out_ref):
    rows = x_ref.shape[0]
    x = jnp.concatenate([part.astype(F32) for part in split(x_ref[...], 3)], axis=0).astype(BF16)
    high, middle, low = (nt(down_ref[part], x) for part in range(3))
    total = high[:, :rows] + (
        (high[:, rows : 2 * rows] + middle[:, :rows])
        + (high[:, 2 * rows :] + middle[:, rows : 2 * rows] + low[:, :rows])
    )
    normed(total.T, gain_ref[...], out_ref)


def latent_kernel(x_ref, down_ref, gain_ref, out_ref):
    down = six(split(x_ref[...], 3), [down_ref[part] for part in range(3)], nt)
    normed(down, gain_ref[...], out_ref)


def query_kernel(x_ref, own_ref, other_ref, out_ref):
    x = split(x_ref[...], 3)
    out_ref[0] = six(x, split(own_ref[...], 3), nt)
    out_ref[1] = six(x, split(other_ref[...], 3), nt)


def block_offset(place, row, cls, rows):
    return (place * 2 + cls) * rows + row


def attend_kernel(rows, scale, blocks, place_ref, *refs):
    mine_ref, theirs_ref, key_ref, value_ref = refs[:4]
    near_refs, far_ref = refs[4:-3], refs[-3]
    out_refs = refs[-2:]
    ctx, core = place_ref[0], place_ref[1]
    rank = key_ref.shape[1]
    heads = mine_ref.shape[0]
    half = mine_ref.shape[1]
    nope = key_ref.shape[2] // heads
    vdim = value_ref.shape[2] // heads
    count = 2 * half

    row = lax.broadcasted_iota(jnp.int32, (count, 1), 0)
    row_cls = jnp.where(row < half, core, 1 - core)
    within = lax.rem(row, half)
    q_pos = ctx * count + block_offset(within // rows, lax.rem(within, rows), row_cls, rows)

    latent = jnp.concatenate([ref[...] for ref in near_refs] + [far_ref[...]], axis=0)
    column = lax.broadcasted_iota(jnp.int32, (1, latent.shape[0]), 1)
    far_column = column - half * len(near_refs)
    step = FAR[0] + lax.rem(far_column // rows, len(FAR))
    within = far_column // (rows * len(FAR)) * rows + lax.rem(column, rows)
    for number, behind in enumerate((0, *RING)):
        inside = column // half == number
        step = jnp.where(inside, behind, step)
        within = jnp.where(inside, column - number * half, within)
    block = lax.rem(ctx - step + blocks, blocks)
    k_pos = block * count + block_offset(within // rows, lax.rem(within, rows), core, rows)
    causal = q_pos >= k_pos

    compressed = split(latent[:, :rank], 3)
    keys = six(compressed, [key_ref[part] for part in range(3)], nn)
    values = three(compressed, [value_ref[part] for part in range(2)], nn)
    for head in range(heads):
        key = jnp.concatenate([keys[:, head * nope : (head + 1) * nope], latent[:, rank:]], axis=1)
        query = jnp.concatenate([mine_ref[head], theirs_ref[heads - 1 - head]], axis=0)
        scores = jnp.where(causal, six(split(query, 3), split(key, 3), nt) * scale, FLOOR)
        top = jnp.max(scores, axis=1, keepdims=True)
        weight = jnp.where(causal, jnp.exp(scores - top), 0.0)
        total = jnp.sum(weight, axis=1, keepdims=True)
        value = split(values[:, head * vdim : (head + 1) * vdim], 2)
        acc = three(split(weight, 2), value, nn)
        for number, out_ref in enumerate(out_refs):
            chosen = slice(number * half, (number + 1) * half)
            out_ref[head, :, :vdim] = acc[chosen]
            out_ref[head, :, vdim : vdim + 64] = jnp.broadcast_to(top[chosen], (half, 64))
            out_ref[head, :, vdim + 64 :] = jnp.broadcast_to(total[chosen], (half, 64))


def share_kernel(state_ref, arrived_ref, out_w_ref, out_ref):
    heads = state_ref.shape[0]
    vdim = out_w_ref.shape[1] // heads
    attended = []
    for head in range(heads):
        mine = state_ref[head]
        other = arrived_ref[heads - 1 - head]
        m0, m1 = mine[:, vdim : vdim + 1], other[:, vdim : vdim + 1]
        top = jnp.maximum(m0, m1)
        f0, f1 = jnp.exp(m0 - top), jnp.exp(m1 - top)
        total = mine[:, vdim + 64 : vdim + 65] * f0 + other[:, vdim + 64 : vdim + 65] * f1
        attended.append((mine[:, :vdim] * f0 + other[:, :vdim] * f1) / total)
    left = split(jnp.concatenate(attended, axis=1), 2)
    out_ref[...] = three(left, [out_w_ref[part] for part in range(2)], nn)


def key_value_kernel(key_ref, far_key_ref, value_ref, far_value_ref, keys_ref, values_ref):
    nope, vdim = key_ref.shape[1], value_ref.shape[1]
    for number, ref in enumerate((key_ref, far_key_ref)):
        for part, value in enumerate(split(ref[...], 3)):
            keys_ref[part, :, number * nope : (number + 1) * nope] = value
    for number, ref in enumerate((value_ref, far_value_ref)):
        for part, value in enumerate(split(ref[...], 2)):
            values_ref[part, :, number * vdim : (number + 1) * vdim] = value


def partner(array):
    size = lax.axis_size("head")
    return lax.ppermute(array, "head", [(h, h ^ 1) for h in range(size)])


def from_behind(array, step):
    size = lax.axis_size("ctx")
    return lax.ppermute(array, "ctx", [(c, (c + step) % size) for c in range(size)])


def exchange(pieces):
    size = lax.axis_size("head")
    groups = [list(range(core, size, 2)) for core in range(2)]
    return lax.all_to_all(
        pieces, "head", split_axis=0, concat_axis=0, tiled=True, axis_index_groups=groups
    )


def spread_kernel(*refs):
    out_ref = refs[-1]
    for number, ref in enumerate(refs[:-1]):
        for copy in range(out_ref.shape[0]):
            out_ref[copy, number] = ref[...]


def spread(array, places):
    return exchange(jnp.broadcast_to(array[None], (places, *array.shape)))


def on_device(hidden, w_query, w_down, latent_gain, w_key_up, w_value_up, w_out):
    rows, depth = hidden.shape
    blocks = lax.axis_size("ctx")
    places = lax.axis_size("head") // 2
    half = places * rows
    rank, nope = w_key_up.shape
    vdim = w_value_up.shape[1]
    width = w_down.shape[1]
    place = jnp.stack([lax.axis_index("ctx"), lax.axis_index("head") & 1]).astype(jnp.int32)
    gain = latent_gain[None]

    mine = spread(hidden, places).reshape(half, depth)
    far_query, far_key, far_value, far_out = (
        partner(weight) for weight in (w_query, w_key_up, w_value_up, w_out)
    )
    down_parts = call(
        functools.partial(split_kernel, 3),
        shape(3, width, depth, dtype=BF16),
        [w_down.T],
        "down_parts",
    )
    own = call(own_kernel, shape(rows, width), [hidden, down_parts, gain], "own_latent")
    far = [from_behind(own, step) for step in FAR]
    far_copies = call(spread_kernel, shape(places, len(FAR), rows, width), far, "far_copies")
    far_latent = exchange(far_copies).reshape(-1, width)

    latent = call(latent_kernel, shape(half, width), [mine, down_parts, gain], "latent")
    ring = [from_behind(latent, step) for step in RING]

    mine, far_query, _ = lax.optimization_barrier((mine, far_query, latent))
    queries = call(
        query_kernel,
        shape(2, half, w_query.shape[1]),
        [mine, w_query.T, far_query.T],
        "query",
    )
    other_queries = partner(queries)
    key_parts, value_parts = call(
        key_value_kernel,
        [shape(3, rank, 2 * nope, dtype=BF16), shape(2, rank, 2 * vdim, dtype=BF16)],
        [w_key_up, far_key, w_value_up, far_value],
        "key_value_parts",
    )
    out_parts = call(
        functools.partial(split_kernel, 2),
        shape(2, 2 * vdim, depth, dtype=BF16),
        [w_out, far_out],
        "out_parts",
    )

    state = call(
        functools.partial(attend_kernel, rows, w_query.shape[1] ** (-0.5), blocks),
        [shape(2, half, 2 * vdim)] * 2,
        [queries, other_queries, key_parts, value_parts, latent, *ring, far_latent],
        "attend",
        place,
    )
    arrived = partner(state[1])
    shares = call(share_kernel, shape(half, depth), [state[0], arrived, out_parts], "share")
    return exchange(shares.reshape(places, rows, depth)).sum(axis=0)


def solution(mesh):
    placed = (
        P(("ctx", "head"), None),
        P(None, "head"),
        P(),
        P(),
        P(None, "head"),
        P(None, "head"),
        P("head", None),
    )
    return jax.shard_map(
        on_device, mesh=mesh, in_specs=placed, out_specs=P(("ctx", "head"), None), check_vma=False
    )
```

```python
import functools

import jax
import jax.numpy as jnp
from jax import lax
from jax.experimental import pallas as pl
from jax.experimental.pallas import tpu as pltpu
from jax.sharding import PartitionSpec as P

EPSILON = 1e-06
FLOOR = -1e30
LOG2E = 1.4426950408889634
RING = (1, -1)
FAR = (2, 3, 4, 5, 6)
F32 = jnp.float32
BF16 = jnp.bfloat16
VMEM = pltpu.VMEM
LIMIT = 24 << 20


def nn(left, right):
    return lax.dot_general(left, right, (((1,), (0,)), ((), ())), preferred_element_type=F32)


def nt(left, right):
    return lax.dot_general(left, right, (((1,), (1,)), ((), ())), preferred_element_type=F32)


def split(array, count):
    parts = []
    for _ in range(count - 1):
        part = array.astype(BF16)
        parts.append(part)
        array = array - part.astype(F32)
    parts.append(array.astype(BF16))
    return parts


def six(left, right, dot):
    high, middle, low = left
    rows = high.shape[0]
    by_high = dot(jnp.concatenate([high, middle, low], axis=0), right[0])
    by_middle = dot(jnp.concatenate([high, middle], axis=0), right[1])
    by_low = dot(high, right[2])
    return by_high[:rows] + (
        (by_high[rows : 2 * rows] + by_middle[:rows])
        + (by_high[2 * rows :] + by_middle[rows:] + by_low)
    )


def three(left, right, dot):
    return dot(left[1], right[0]) + dot(left[0], right[1]) + dot(left[0], right[0])


def call(kernel, outs, operands, name, place=None):
    first = [] if place is None else [place]
    return pl.pallas_call(
        kernel,
        out_shape=outs,
        in_specs=[pl.BlockSpec(memory_space=pltpu.SMEM)] * len(first)
        + [pl.BlockSpec(memory_space=VMEM)] * len(operands),
        out_specs=jax.tree.map(lambda _: pl.BlockSpec(memory_space=VMEM), outs),
        compiler_params=pltpu.CompilerParams(vmem_limit_bytes=LIMIT),
        name=name,
    )(*first, *operands)


def shape(*dims, dtype=F32):
    return jax.ShapeDtypeStruct(dims, dtype)


def split_kernel(count, *refs):
    sources, outs = refs[:-1], refs[-1]
    start = 0
    for ref in sources:
        stop = start + ref.shape[0]
        for part, value in enumerate(split(ref[...], count)):
            outs[part, start:stop] = value
        start = stop


def normed(down, gain, out_ref):
    rank = gain.shape[1]
    raw = down[:, :rank]
    meansq = jnp.mean(raw * raw, axis=-1, keepdims=True)
    out_ref[:, :rank] = raw * lax.rsqrt(meansq + EPSILON) * gain
    out_ref[:, rank:] = down[:, rank:]


def own_kernel(x_ref, down_ref, gain_ref, out_ref):
    rows = x_ref.shape[0]
    x = jnp.concatenate([part.astype(F32) for part in split(x_ref[...], 3)], axis=0).astype(BF16)
    high, middle, low = (nt(part, x) for part in split(down_ref[...], 3))
    total = high[:, :rows] + (
        (high[:, rows : 2 * rows] + middle[:, :rows])
        + (high[:, 2 * rows :] + middle[:, rows : 2 * rows] + low[:, :rows])
    )
    normed(total.T, gain_ref[...], out_ref)


def latent_kernel(x_ref, down_ref, gain_ref, out_ref):
    down = six(split(x_ref[...], 3), split(down_ref[...], 3), nt)
    normed(down, gain_ref[...], out_ref)


def query_kernel(x_ref, own_ref, other_ref, out_ref):
    x = split(x_ref[...], 3)
    out_ref[0] = six(x, split(own_ref[...], 3), nt)
    out_ref[1] = six(x, split(other_ref[...], 3), nt)


def block_offset(place, row, cls, rows):
    return (place * 2 + cls) * rows + row


def attend_kernel(rows, scale, blocks, place_ref, *refs):
    mine_ref, theirs_ref, key_ref, far_key_ref, value_ref, far_value_ref = refs[:6]
    near_refs, far_ref = refs[6:-3], refs[-3]
    out_refs = refs[-2:]
    ctx, core = place_ref[0], place_ref[1]
    rank, nope = key_ref.shape
    vdim = value_ref.shape[1]
    heads, half, _ = mine_ref.shape
    count = 2 * half

    row = lax.broadcasted_iota(jnp.int32, (count, 1), 0)
    row_cls = jnp.where(row < half, core, 1 - core)
    within = lax.rem(row, half)
    q_pos = ctx * count + block_offset(within // rows, lax.rem(within, rows), row_cls, rows)

    latent = jnp.concatenate([ref[...] for ref in near_refs] + [far_ref[...]], axis=0)
    column = lax.broadcasted_iota(jnp.int32, (1, latent.shape[0]), 1)
    far_column = column - half * len(near_refs)
    step = FAR[0] + lax.rem(far_column // rows, len(FAR))
    within = far_column // (rows * len(FAR)) * rows + lax.rem(column, rows)
    for number, behind in enumerate((0, *RING)):
        inside = column // half == number
        step = jnp.where(inside, behind, step)
        within = jnp.where(inside, column - number * half, within)
    block = lax.rem(ctx - step + blocks, blocks)
    k_pos = block * count + block_offset(within // rows, lax.rem(within, rows), core, rows)
    causal = q_pos >= k_pos

    compressed = split(latent[:, :rank], 2)
    key_up = jnp.concatenate([key_ref[...], far_key_ref[...]], axis=1)
    value_up = jnp.concatenate([value_ref[...], far_value_ref[...]], axis=1)
    keys = three(compressed, split(key_up, 2), nn)
    values = three(compressed, split(value_up, 2), nn)
    high, middle, low = split(latent[:, rank:], 3)
    shared_keys = [high, middle, low, high, middle, high]
    for head in range(heads):
        high, low = split(keys[:, head * nope : (head + 1) * nope], 2)
        key = jnp.concatenate([high, low, high, *shared_keys], axis=1)
        query = jnp.concatenate([mine_ref[head], theirs_ref[heads - 1 - head]], axis=0)
        query = query * (scale * LOG2E)
        high, low = split(query[:, :nope], 2)
        own_queries = [low, high, high]
        high, middle, low = split(query[:, nope:], 3)
        shared_queries = [low, middle, high, middle, high, high]
        scores = nt(jnp.concatenate(own_queries + shared_queries, axis=1), key)
        scores = jnp.where(causal, scores, FLOOR)
        top = jnp.max(scores, axis=1, keepdims=True)
        weight = jnp.exp2(scores - top)
        total = jnp.sum(weight, axis=1, keepdims=True)
        value = split(values[:, head * vdim : (head + 1) * vdim], 2)
        acc = three(split(weight, 2), value, nn)
        for number, out_ref in enumerate(out_refs):
            chosen = slice(number * half, (number + 1) * half)
            out_ref[head, :, :vdim] = acc[chosen]
            out_ref[head, :, vdim : vdim + 64] = jnp.broadcast_to(top[chosen], (half, 64))
            out_ref[head, :, vdim + 64 :] = jnp.broadcast_to(total[chosen], (half, 64))


def share_kernel(state_ref, arrived_ref, out_w_ref, out_ref):
    heads = state_ref.shape[0]
    vdim = out_w_ref.shape[1] // heads
    attended = []
    for head in range(heads):
        mine = state_ref[head]
        other = arrived_ref[heads - 1 - head]
        m0, m1 = mine[:, vdim : vdim + 1], other[:, vdim : vdim + 1]
        top = jnp.maximum(m0, m1)
        f0, f1 = jnp.exp2(m0 - top), jnp.exp2(m1 - top)
        total = mine[:, vdim + 64 : vdim + 65] * f0 + other[:, vdim + 64 : vdim + 65] * f1
        attended.append((mine[:, :vdim] * f0 + other[:, :vdim] * f1) / total)
    left = split(jnp.concatenate(attended, axis=1), 2)
    out_ref[...] = three(left, [out_w_ref[part] for part in range(2)], nn)


def partner(array):
    size = lax.axis_size("head")
    return lax.ppermute(array, "head", [(h, h ^ 1) for h in range(size)])


def from_behind(array, step):
    size = lax.axis_size("ctx")
    return lax.ppermute(array, "ctx", [(c, (c + step) % size) for c in range(size)])


def exchange(pieces):
    size = lax.axis_size("head")
    groups = [list(range(core, size, 2)) for core in range(2)]
    return lax.all_to_all(
        pieces, "head", split_axis=0, concat_axis=0, tiled=True, axis_index_groups=groups
    )


def spread_kernel(*refs):
    out_ref = refs[-1]
    for number, ref in enumerate(refs[:-1]):
        for copy in range(out_ref.shape[0]):
            out_ref[copy, number] = ref[...]


def spread(array, places):
    return exchange(jnp.broadcast_to(array[None], (places, *array.shape)))


def on_device(hidden, w_query, w_down, latent_gain, w_key_up, w_value_up, w_out):
    rows, depth = hidden.shape
    blocks = lax.axis_size("ctx")
    places = lax.axis_size("head") // 2
    half = places * rows
    vdim = w_value_up.shape[1]
    width = w_down.shape[1]
    place = jnp.stack([lax.axis_index("ctx"), lax.axis_index("head") & 1]).astype(jnp.int32)
    gain = latent_gain[None]

    mine = spread(hidden, places).reshape(half, depth)
    far_query, far_key, far_value, far_out = (
        partner(weight) for weight in (w_query, w_key_up, w_value_up, w_out)
    )
    own = call(own_kernel, shape(rows, width), [hidden, w_down.T, gain], "own_latent")
    far = [from_behind(own, step) for step in FAR]
    far_copies = call(spread_kernel, shape(places, len(FAR), rows, width), far, "far_copies")
    far_latent = exchange(far_copies).reshape(-1, width)

    latent = call(latent_kernel, shape(half, width), [mine, w_down.T, gain], "latent")
    ring = [from_behind(latent, step) for step in RING]

    mine, far_query, _ = lax.optimization_barrier((mine, far_query, latent))
    queries = call(
        query_kernel,
        shape(2, half, w_query.shape[1]),
        [mine, w_query.T, far_query.T],
        "query",
    )
    other_queries = partner(queries)
    out_parts = call(
        functools.partial(split_kernel, 2),
        shape(2, 2 * vdim, depth, dtype=BF16),
        [w_out, far_out],
        "out_parts",
    )

    latent, out_parts = lax.optimization_barrier((latent, out_parts))
    state = call(
        functools.partial(attend_kernel, rows, w_query.shape[1] ** (-0.5), blocks),
        [shape(2, half, 2 * vdim)] * 2,
        [
            queries,
            other_queries,
            w_key_up,
            far_key,
            w_value_up,
            far_value,
            latent,
            *ring,
            far_latent,
        ],
        "attend",
        place,
    )
    arrived = partner(state[1])
    shares = call(share_kernel, shape(half, depth), [state[0], arrived, out_parts], "share")
    return exchange(shares.reshape(places, rows, depth)).sum(axis=0)


def solution(mesh):
    placed = (
        P(("ctx", "head"), None),
        P(None, "head"),
        P(),
        P(),
        P(None, "head"),
        P(None, "head"),
        P("head", None),
    )
    return jax.shard_map(
        on_device, mesh=mesh, in_specs=placed, out_specs=P(("ctx", "head"), None), check_vma=False
    )
```

```python
import functools

import jax
import jax.numpy as jnp
from jax import lax
from jax.experimental import pallas as pl
from jax.experimental.pallas import tpu as pltpu
from jax.sharding import PartitionSpec as P

EPSILON = 1e-06
FLOOR = -1e30
LOG2E = 1.4426950408889634
RING = (1, -1)
FAR = (2, 3, 4, 5, 6)
F32 = jnp.float32
BF16 = jnp.bfloat16
VMEM = pltpu.VMEM
LIMIT = 24 << 20


def nn(left, right):
    return lax.dot_general(left, right, (((1,), (0,)), ((), ())), preferred_element_type=F32)


def nt(left, right):
    return lax.dot_general(left, right, (((1,), (1,)), ((), ())), preferred_element_type=F32)


def split(array):
    high = array.astype(BF16)
    return high, (array - high.astype(F32)).astype(BF16)


def product(left, right, dot):
    return dot(left[1], right[0]) + dot(left[0], right[1]) + dot(left[0], right[0])


def stacked(left, right, dot):
    rows = left[0].shape[0]
    by_high = dot(jnp.concatenate(left, axis=0), right[0])
    return by_high[:rows] + (by_high[rows:] + dot(left[0], right[1]))


def call(kernel, outs, operands, name, place=None):
    first = [] if place is None else [place]
    return pl.pallas_call(
        kernel,
        out_shape=outs,
        in_specs=[pl.BlockSpec(memory_space=pltpu.SMEM)] * len(first)
        + [pl.BlockSpec(memory_space=VMEM)] * len(operands),
        out_specs=jax.tree.map(lambda _: pl.BlockSpec(memory_space=VMEM), outs),
        compiler_params=pltpu.CompilerParams(vmem_limit_bytes=LIMIT),
        name=name,
    )(*first, *operands)


def shape(*dims, dtype=F32):
    return jax.ShapeDtypeStruct(dims, dtype)


def split_kernel(*refs):
    sources, outs = refs[:-1], refs[-1]
    start = 0
    for ref in sources:
        stop = start + ref.shape[0]
        outs[0, start:stop], outs[1, start:stop] = split(ref[...])
        start = stop


def normed(down, gain, out_ref):
    rank = gain.shape[1]
    raw = down[:, :rank]
    meansq = jnp.mean(raw * raw, axis=-1, keepdims=True)
    out_ref[:, :rank] = raw * lax.rsqrt(meansq + EPSILON) * gain
    out_ref[:, rank:] = down[:, rank:]


def own_kernel(x_ref, down_ref, gain_ref, out_ref):
    rows = x_ref.shape[0]
    x = jnp.concatenate([part.astype(F32) for part in split(x_ref[...])], axis=0).astype(BF16)
    high, low = (nt(part, x) for part in split(down_ref[...]))
    total = high[:, :rows] + (high[:, rows:] + low[:, :rows])
    normed(total.T, gain_ref[...], out_ref)


def latent_kernel(x_ref, down_ref, gain_ref, out_ref):
    down = stacked(split(x_ref[...]), split(down_ref[...]), nt)
    normed(down, gain_ref[...], out_ref)


def query_kernel(x_ref, own_ref, other_ref, out_ref):
    x = split(x_ref[...])
    out_ref[0] = stacked(x, split(own_ref[...]), nt)
    out_ref[1] = stacked(x, split(other_ref[...]), nt)


def block_offset(place, row, cls, rows):
    return (place * 2 + cls) * rows + row


def attend_kernel(rows, scale, blocks, place_ref, *refs):
    mine_ref, theirs_ref, key_ref, far_key_ref, value_ref, far_value_ref = refs[:6]
    near_refs, far_ref = refs[6:-3], refs[-3]
    out_refs = refs[-2:]
    ctx, core = place_ref[0], place_ref[1]
    rank, nope = key_ref.shape
    vdim = value_ref.shape[1]
    heads, half, _ = mine_ref.shape
    count = 2 * half

    row = lax.broadcasted_iota(jnp.int32, (count, 1), 0)
    row_cls = jnp.where(row < half, core, 1 - core)
    within = lax.rem(row, half)
    q_pos = ctx * count + block_offset(within // rows, lax.rem(within, rows), row_cls, rows)

    latent = jnp.concatenate([ref[...] for ref in near_refs] + [far_ref[...]], axis=0)
    column = lax.broadcasted_iota(jnp.int32, (1, latent.shape[0]), 1)
    far_column = column - half * len(near_refs)
    step = FAR[0] + lax.rem(far_column // rows, len(FAR))
    within = far_column // (rows * len(FAR)) * rows + lax.rem(column, rows)
    for number, behind in enumerate((0, *RING)):
        inside = column // half == number
        step = jnp.where(inside, behind, step)
        within = jnp.where(inside, column - number * half, within)
    block = lax.rem(ctx - step + blocks, blocks)
    k_pos = block * count + block_offset(within // rows, lax.rem(within, rows), core, rows)
    causal = q_pos >= k_pos

    high, low = split(latent)
    compressed = high[:, :rank], low[:, :rank]
    key_up = jnp.concatenate([key_ref[...], far_key_ref[...]], axis=1)
    value_up = jnp.concatenate([value_ref[...], far_value_ref[...]], axis=1)
    keys = split(product(compressed, split(key_up), nn))
    values = split(product(compressed, split(value_up), nn))
    shared = high[:, rank:], low[:, rank:]
    for head in range(heads):
        high, low = (
            jnp.concatenate([own[:, head * nope : (head + 1) * nope], other], axis=1)
            for own, other in zip(keys, shared)
        )
        key = jnp.concatenate([high, low, high], axis=1)
        query = jnp.concatenate([mine_ref[head], theirs_ref[heads - 1 - head]], axis=0)
        high, low = split(query * (scale * LOG2E))
        scores = nt(jnp.concatenate([low, high, high], axis=1), key)
        scores = jnp.where(causal, scores, FLOOR)
        top = jnp.max(scores, axis=1, keepdims=True)
        weight = jnp.exp2(scores - top)
        total = jnp.sum(weight, axis=1, keepdims=True)
        acc = product(
            split(weight), [part[:, head * vdim : (head + 1) * vdim] for part in values], nn
        )
        for number, out_ref in enumerate(out_refs):
            chosen = slice(number * half, (number + 1) * half)
            out_ref[head, :, :vdim] = acc[chosen]
            out_ref[head, :, vdim : vdim + 64] = jnp.broadcast_to(top[chosen], (half, 64))
            out_ref[head, :, vdim + 64 :] = jnp.broadcast_to(total[chosen], (half, 64))


def share_kernel(state_ref, arrived_ref, out_w_ref, out_ref):
    heads = state_ref.shape[0]
    vdim = out_w_ref.shape[1] // heads
    attended = []
    for head in range(heads):
        mine = state_ref[head]
        other = arrived_ref[heads - 1 - head]
        m0, m1 = mine[:, vdim : vdim + 1], other[:, vdim : vdim + 1]
        top = jnp.maximum(m0, m1)
        f0, f1 = jnp.exp2(m0 - top), jnp.exp2(m1 - top)
        total = mine[:, vdim + 64 : vdim + 65] * f0 + other[:, vdim + 64 : vdim + 65] * f1
        attended.append((mine[:, :vdim] * f0 + other[:, :vdim] * f1) / total)
    left = split(jnp.concatenate(attended, axis=1))
    out_ref[...] = stacked(left, [out_w_ref[part] for part in range(2)], nn)


def partner(array):
    size = lax.axis_size("head")
    return lax.ppermute(array, "head", [(h, h ^ 1) for h in range(size)])


def from_behind(array, step):
    size = lax.axis_size("ctx")
    return lax.ppermute(array, "ctx", [(c, (c + step) % size) for c in range(size)])


def exchange(pieces):
    size = lax.axis_size("head")
    groups = [list(range(core, size, 2)) for core in range(2)]
    return lax.all_to_all(
        pieces, "head", split_axis=0, concat_axis=0, tiled=True, axis_index_groups=groups
    )


def spread_kernel(*refs):
    out_ref = refs[-1]
    for number, ref in enumerate(refs[:-1]):
        for copy in range(out_ref.shape[0]):
            out_ref[copy, number] = ref[...]


def spread(array, places):
    return exchange(jnp.broadcast_to(array[None], (places, *array.shape)))


def on_device(hidden, w_query, w_down, latent_gain, w_key_up, w_value_up, w_out):
    rows, depth = hidden.shape
    blocks = lax.axis_size("ctx")
    places = lax.axis_size("head") // 2
    half = places * rows
    vdim = w_value_up.shape[1]
    width = w_down.shape[1]
    place = jnp.stack([lax.axis_index("ctx"), lax.axis_index("head") & 1]).astype(jnp.int32)
    gain = latent_gain[None]

    mine = spread(hidden, places).reshape(half, depth)
    far_query, far_key, far_value, far_out = (
        partner(weight) for weight in (w_query, w_key_up, w_value_up, w_out)
    )
    own = call(own_kernel, shape(rows, width), [hidden, w_down.T, gain], "own_latent")
    far = [from_behind(own, step) for step in FAR]
    far, far_out = lax.optimization_barrier((far, far_out))
    far_copies = call(spread_kernel, shape(places, len(FAR), rows, width), far, "far_copies")
    far_latent = exchange(far_copies).reshape(-1, width)

    latent = call(latent_kernel, shape(half, width), [mine, w_down.T, gain], "latent")
    ring = [from_behind(latent, step) for step in RING]

    mine, far_query, _ = lax.optimization_barrier((mine, far_query, latent))
    queries = call(
        query_kernel,
        shape(2, half, w_query.shape[1]),
        [mine, w_query.T, far_query.T],
        "query",
    )
    other_queries = partner(queries)
    out_parts = call(
        split_kernel,
        shape(2, 2 * vdim, depth, dtype=BF16),
        [w_out, far_out],
        "out_parts",
    )

    latent, out_parts = lax.optimization_barrier((latent, out_parts))
    state = call(
        functools.partial(attend_kernel, rows, w_query.shape[1] ** (-0.5), blocks),
        [shape(2, half, 2 * vdim)] * 2,
        [
            queries,
            other_queries,
            w_key_up,
            far_key,
            w_value_up,
            far_value,
            latent,
            *ring,
            far_latent,
        ],
        "attend",
        place,
    )
    arrived = partner(state[1])
    shares = call(share_kernel, shape(half, depth), [state[0], arrived, out_parts], "share")
    return exchange(shares.reshape(places, rows, depth)).sum(axis=0)


def solution(mesh):
    placed = (
        P(("ctx", "head"), None),
        P(None, "head"),
        P(),
        P(),
        P(None, "head"),
        P(None, "head"),
        P("head", None),
    )
    return jax.shard_map(
        on_device, mesh=mesh, in_specs=placed, out_specs=P(("ctx", "head"), None), check_vma=False
    )
```

```python
import functools

import jax
import jax.numpy as jnp
from jax import lax
from jax.experimental import pallas as pl
from jax.experimental.pallas import tpu as pltpu
from jax.sharding import PartitionSpec as P

EPSILON = 1e-06
FLOOR = -1e30
LOG2E = 1.4426950408889634
RING = (1, -1)
FAR = (2, 3, 4, 5, 6)
F32 = jnp.float32
BF16 = jnp.bfloat16
VMEM = pltpu.VMEM
LIMIT = 24 << 20


def nn(left, right):
    return lax.dot_general(left, right, (((1,), (0,)), ((), ())), preferred_element_type=F32)


def nt(left, right):
    return lax.dot_general(left, right, (((1,), (1,)), ((), ())), preferred_element_type=F32)


def split(array, count):
    parts = []
    for _ in range(count - 1):
        part = array.astype(BF16)
        parts.append(part)
        array = array - part.astype(F32)
    parts.append(array.astype(BF16))
    return parts


def six(left, right, dot):
    high, middle, low = left
    rows = high.shape[0]
    by_high = dot(jnp.concatenate([high, middle, low], axis=0), right[0])
    by_middle = dot(jnp.concatenate([high, middle], axis=0), right[1])
    by_low = dot(high, right[2])
    return by_high[:rows] + (
        (by_high[rows : 2 * rows] + by_middle[:rows])
        + (by_high[2 * rows :] + by_middle[rows:] + by_low)
    )


def three(left, right, dot):
    return dot(left[1], right[0]) + dot(left[0], right[1]) + dot(left[0], right[0])


def call(kernel, outs, operands, name, place=None):
    first = [] if place is None else [place]
    return pl.pallas_call(
        kernel,
        out_shape=outs,
        in_specs=[pl.BlockSpec(memory_space=pltpu.SMEM)] * len(first)
        + [pl.BlockSpec(memory_space=VMEM)] * len(operands),
        out_specs=jax.tree.map(lambda _: pl.BlockSpec(memory_space=VMEM), outs),
        compiler_params=pltpu.CompilerParams(vmem_limit_bytes=LIMIT),
        name=name,
    )(*first, *operands)


def shape(*dims, dtype=F32):
    return jax.ShapeDtypeStruct(dims, dtype)


def split_kernel(count, *refs):
    sources, outs = refs[:-1], refs[-1]
    start = 0
    for ref in sources:
        stop = start + ref.shape[0]
        for part, value in enumerate(split(ref[...], count)):
            outs[part, start:stop] = value
        start = stop


def normed(down, gain, out_ref):
    rank = gain.shape[1]
    raw = down[:, :rank]
    meansq = jnp.mean(raw * raw, axis=-1, keepdims=True)
    out_ref[:, :rank] = raw * lax.rsqrt(meansq + EPSILON) * gain
    out_ref[:, rank:] = down[:, rank:]


def own_kernel(x_ref, down_ref, gain_ref, out_ref):
    rows = x_ref.shape[0]
    x = jnp.concatenate([part.astype(F32) for part in split(x_ref[...], 3)], axis=0).astype(BF16)
    rank = gain_ref.shape[1]
    high, low = (nt(part, x) for part in split(down_ref[:rank], 2))
    raw = high[:, :rows] + (high[:, rows : 2 * rows] + low[:, :rows])
    high, middle, low = (nt(part, x) for part in split(down_ref[rank:], 3))
    shared = high[:, :rows] + (
        (high[:, rows : 2 * rows] + middle[:, :rows])
        + (high[:, 2 * rows :] + middle[:, rows : 2 * rows] + low[:, :rows])
    )
    normed(jnp.concatenate([raw, shared], axis=0).T, gain_ref[...], out_ref)


def latent_kernel(x_ref, down_ref, gain_ref, out_ref):
    rank = gain_ref.shape[1]
    x = split(x_ref[...], 3)
    rows = x_ref.shape[0]
    high, low = split(down_ref[:rank], 2)
    by_high = nt(jnp.concatenate(x[:2], axis=0), high)
    raw = by_high[:rows] + (by_high[rows:] + nt(x[0], low))
    shared = six(x, split(down_ref[rank:], 3), nt)
    normed(jnp.concatenate([raw, shared], axis=1), gain_ref[...], out_ref)


def query_kernel(x_ref, own_ref, other_ref, out_ref):
    x = split(x_ref[...], 3)
    out_ref[0] = six(x, split(own_ref[...], 3), nt)
    out_ref[1] = six(x, split(other_ref[...], 3), nt)


def block_offset(place, row, cls, rows):
    return (place * 2 + cls) * rows + row


def attend_kernel(rows, scale, blocks, place_ref, *refs):
    mine_ref, theirs_ref, key_ref, far_key_ref, value_ref, far_value_ref = refs[:6]
    near_refs, far_ref = refs[6:-3], refs[-3]
    out_refs = refs[-2:]
    ctx, core = place_ref[0], place_ref[1]
    rank, nope = key_ref.shape
    vdim = value_ref.shape[1]
    heads, half, _ = mine_ref.shape
    count = 2 * half

    row = lax.broadcasted_iota(jnp.int32, (count, 1), 0)
    row_cls = jnp.where(row < half, core, 1 - core)
    within = lax.rem(row, half)
    q_pos = ctx * count + block_offset(within // rows, lax.rem(within, rows), row_cls, rows)

    latent = jnp.concatenate([ref[...] for ref in near_refs] + [far_ref[...]], axis=0)
    column = lax.broadcasted_iota(jnp.int32, (1, latent.shape[0]), 1)
    far_column = column - half * len(near_refs)
    step = FAR[0] + lax.rem(far_column // rows, len(FAR))
    within = far_column // (rows * len(FAR)) * rows + lax.rem(column, rows)
    for number, behind in enumerate((0, *RING)):
        inside = column // half == number
        step = jnp.where(inside, behind, step)
        within = jnp.where(inside, column - number * half, within)
    block = lax.rem(ctx - step + blocks, blocks)
    k_pos = block * count + block_offset(within // rows, lax.rem(within, rows), core, rows)
    causal = q_pos >= k_pos

    compressed = split(latent[:, :rank], 2)
    key_up = jnp.concatenate([key_ref[...], far_key_ref[...]], axis=1)
    value_up = jnp.concatenate([value_ref[...], far_value_ref[...]], axis=1)
    keys = three(compressed, split(key_up, 2), nn)
    values = three(compressed, split(value_up, 2), nn)
    high, middle, low = split(latent[:, rank:], 3)
    shared_keys = [high, middle, low, high, middle, high]
    for head in range(heads):
        high, low = split(keys[:, head * nope : (head + 1) * nope], 2)
        key = jnp.concatenate([high, low, high, *shared_keys], axis=1)
        query = jnp.concatenate([mine_ref[head], theirs_ref[heads - 1 - head]], axis=0)
        query = query * (scale * LOG2E)
        high, low = split(query[:, :nope], 2)
        own_queries = [low, high, high]
        high, middle, low = split(query[:, nope:], 3)
        shared_queries = [low, middle, high, middle, high, high]
        scores = nt(jnp.concatenate(own_queries + shared_queries, axis=1), key)
        scores = jnp.where(causal, scores, FLOOR)
        top = jnp.max(scores, axis=1, keepdims=True)
        weight = jnp.exp2(scores - top)
        total = jnp.sum(weight, axis=1, keepdims=True)
        value = split(values[:, head * vdim : (head + 1) * vdim], 2)
        acc = three(split(weight, 2), value, nn)
        for number, out_ref in enumerate(out_refs):
            chosen = slice(number * half, (number + 1) * half)
            out_ref[head, :, :vdim] = acc[chosen]
            out_ref[head, :, vdim : vdim + 64] = jnp.broadcast_to(top[chosen], (half, 64))
            out_ref[head, :, vdim + 64 :] = jnp.broadcast_to(total[chosen], (half, 64))


def share_kernel(state_ref, arrived_ref, out_w_ref, out_ref):
    heads = state_ref.shape[0]
    vdim = out_w_ref.shape[1] // heads
    attended = []
    for head in range(heads):
        mine = state_ref[head]
        other = arrived_ref[heads - 1 - head]
        m0, m1 = mine[:, vdim : vdim + 1], other[:, vdim : vdim + 1]
        top = jnp.maximum(m0, m1)
        f0, f1 = jnp.exp2(m0 - top), jnp.exp2(m1 - top)
        total = mine[:, vdim + 64 : vdim + 65] * f0 + other[:, vdim + 64 : vdim + 65] * f1
        attended.append((mine[:, :vdim] * f0 + other[:, :vdim] * f1) / total)
    left = split(jnp.concatenate(attended, axis=1), 2)
    out_ref[...] = three(left, [out_w_ref[part] for part in range(2)], nn)


def partner(array):
    size = lax.axis_size("head")
    return lax.ppermute(array, "head", [(h, h ^ 1) for h in range(size)])


def from_behind(array, step):
    size = lax.axis_size("ctx")
    return lax.ppermute(array, "ctx", [(c, (c + step) % size) for c in range(size)])


def exchange(pieces):
    size = lax.axis_size("head")
    groups = [list(range(core, size, 2)) for core in range(2)]
    return lax.all_to_all(
        pieces, "head", split_axis=0, concat_axis=0, tiled=True, axis_index_groups=groups
    )


def spread_kernel(*refs):
    out_ref = refs[-1]
    for number, ref in enumerate(refs[:-1]):
        for copy in range(out_ref.shape[0]):
            out_ref[copy, number] = ref[...]


def spread(array, places):
    return exchange(jnp.broadcast_to(array[None], (places, *array.shape)))


def on_device(hidden, w_query, w_down, latent_gain, w_key_up, w_value_up, w_out):
    rows, depth = hidden.shape
    blocks = lax.axis_size("ctx")
    places = lax.axis_size("head") // 2
    half = places * rows
    vdim = w_value_up.shape[1]
    width = w_down.shape[1]
    place = jnp.stack([lax.axis_index("ctx"), lax.axis_index("head") & 1]).astype(jnp.int32)
    gain = latent_gain[None]

    mine = spread(hidden, places).reshape(half, depth)
    far_query, far_key, far_value, far_out = (
        partner(weight) for weight in (w_query, w_key_up, w_value_up, w_out)
    )
    own = call(own_kernel, shape(rows, width), [hidden, w_down.T, gain], "own_latent")
    far = [from_behind(own, step) for step in FAR]
    far, far_out = lax.optimization_barrier((far, far_out))
    far_copies = call(spread_kernel, shape(places, len(FAR), rows, width), far, "far_copies")
    far_latent = exchange(far_copies).reshape(-1, width)

    latent = call(latent_kernel, shape(half, width), [mine, w_down.T, gain], "latent")
    ring = [from_behind(latent, step) for step in RING]

    mine, far_query, _ = lax.optimization_barrier((mine, far_query, latent))
    queries = call(
        query_kernel,
        shape(2, half, w_query.shape[1]),
        [mine, w_query.T, far_query.T],
        "query",
    )
    other_queries = partner(queries)
    out_parts = call(
        functools.partial(split_kernel, 2),
        shape(2, 2 * vdim, depth, dtype=BF16),
        [w_out, far_out],
        "out_parts",
    )

    latent, out_parts = lax.optimization_barrier((latent, out_parts))
    state = call(
        functools.partial(attend_kernel, rows, w_query.shape[1] ** (-0.5), blocks),
        [shape(2, half, 2 * vdim)] * 2,
        [
            queries,
            other_queries,
            w_key_up,
            far_key,
            w_value_up,
            far_value,
            latent,
            *ring,
            far_latent,
        ],
        "attend",
        place,
    )
    arrived = partner(state[1])
    shares = call(share_kernel, shape(half, depth), [state[0], arrived, out_parts], "share")
    return exchange(shares.reshape(places, rows, depth)).sum(axis=0)


def solution(mesh):
    placed = (
        P(("ctx", "head"), None),
        P(None, "head"),
        P(),
        P(),
        P(None, "head"),
        P(None, "head"),
        P("head", None),
    )
    return jax.shard_map(
        on_device, mesh=mesh, in_specs=placed, out_specs=P(("ctx", "head"), None), check_vma=False
    )
```

```python
import functools

import jax
import jax.numpy as jnp
from jax import lax
from jax.experimental import pallas as pl
from jax.experimental.pallas import tpu as pltpu
from jax.sharding import PartitionSpec as P

EPSILON = 1e-06
FLOOR = -1e30
LOG2E = 1.4426950408889634
RING = (1, -1)
FAR = (2, 3, 4, 5, 6)
F32 = jnp.float32
BF16 = jnp.bfloat16
VMEM = pltpu.VMEM
LIMIT = 24 << 20


def nn(left, right):
    return lax.dot_general(left, right, (((1,), (0,)), ((), ())), preferred_element_type=F32)


def nt(left, right):
    return lax.dot_general(left, right, (((1,), (1,)), ((), ())), preferred_element_type=F32)


def split(array, count):
    parts = []
    for _ in range(count - 1):
        part = array.astype(BF16)
        parts.append(part)
        array = array - part.astype(F32)
    parts.append(array.astype(BF16))
    return parts


def six(left, right, dot):
    high, middle, low = left
    rows = high.shape[0]
    by_high = dot(jnp.concatenate([high, middle, low], axis=0), right[0])
    by_middle = dot(jnp.concatenate([high, middle], axis=0), right[1])
    by_low = dot(high, right[2])
    return by_high[:rows] + (
        (by_high[rows : 2 * rows] + by_middle[:rows])
        + (by_high[2 * rows :] + by_middle[rows:] + by_low)
    )


def three(left, right, dot):
    return dot(left[1], right[0]) + dot(left[0], right[1]) + dot(left[0], right[0])


def call(kernel, outs, operands, name, place=None):
    first = [] if place is None else [place]
    return pl.pallas_call(
        kernel,
        out_shape=outs,
        in_specs=[pl.BlockSpec(memory_space=pltpu.SMEM)] * len(first)
        + [pl.BlockSpec(memory_space=VMEM)] * len(operands),
        out_specs=jax.tree.map(lambda _: pl.BlockSpec(memory_space=VMEM), outs),
        compiler_params=pltpu.CompilerParams(vmem_limit_bytes=LIMIT),
        name=name,
    )(*first, *operands)


def shape(*dims, dtype=F32):
    return jax.ShapeDtypeStruct(dims, dtype)


def split_kernel(count, *refs):
    sources, outs = refs[:-1], refs[-1]
    start = 0
    for ref in sources:
        stop = start + ref.shape[0]
        for part, value in enumerate(split(ref[...], count)):
            outs[part, start:stop] = value
        start = stop


def normed(down, gain, out_ref):
    rank = gain.shape[1]
    raw = down[:, :rank]
    meansq = jnp.mean(raw * raw, axis=-1, keepdims=True)
    out_ref[:, :rank] = raw * lax.rsqrt(meansq + EPSILON) * gain
    out_ref[:, rank:] = down[:, rank:]


def own_kernel(x_ref, down_ref, gain_ref, out_ref):
    rows = x_ref.shape[0]
    x = jnp.concatenate([part.astype(F32) for part in split(x_ref[...], 3)], axis=0).astype(BF16)
    rank = gain_ref.shape[1]
    high, low = (nt(part, x) for part in split(down_ref[:rank], 2))
    raw = high[:, :rows] + (high[:, rows : 2 * rows] + low[:, :rows])
    high, middle, low = (nt(part, x) for part in split(down_ref[rank:], 3))
    shared = high[:, :rows] + (
        (high[:, rows : 2 * rows] + middle[:, :rows])
        + (high[:, 2 * rows :] + middle[:, rows : 2 * rows] + low[:, :rows])
    )
    normed(jnp.concatenate([raw, shared], axis=0).T, gain_ref[...], out_ref)


def latent_kernel(x_ref, down_ref, gain_ref, out_ref):
    rank = gain_ref.shape[1]
    x = split(x_ref[...], 3)
    rows = x_ref.shape[0]
    high, low = split(down_ref[:rank], 2)
    by_high = nt(jnp.concatenate(x[:2], axis=0), high)
    raw = by_high[:rows] + (by_high[rows:] + nt(x[0], low))
    shared = six(x, split(down_ref[rank:], 3), nt)
    normed(jnp.concatenate([raw, shared], axis=1), gain_ref[...], out_ref)


def query_kernel(x_ref, own_ref, other_ref, out_ref):
    x = split(x_ref[...], 3)
    out_ref[0] = six(x, split(own_ref[...], 3), nt)
    out_ref[1] = six(x, split(other_ref[...], 3), nt)


def block_offset(place, row, cls, rows):
    return (place * 2 + cls) * rows + row


def attend_kernel(rows, scale, blocks, place_ref, *refs):
    mine_ref, theirs_ref, key_ref, far_key_ref, value_ref, far_value_ref = refs[:6]
    near_refs, far_ref = refs[6:-3], refs[-3]
    out_refs = refs[-2:]
    ctx, core = place_ref[0], place_ref[1]
    rank, nope = key_ref.shape
    vdim = value_ref.shape[1]
    heads, half, _ = mine_ref.shape
    count = 2 * half

    row = lax.broadcasted_iota(jnp.int32, (count, 1), 0)
    row_cls = jnp.where(row < half, core, 1 - core)
    within = lax.rem(row, half)
    q_pos = ctx * count + block_offset(within // rows, lax.rem(within, rows), row_cls, rows)

    latent = jnp.concatenate([ref[...] for ref in near_refs] + [far_ref[...]], axis=0)
    column = lax.broadcasted_iota(jnp.int32, (1, latent.shape[0]), 1)
    far_column = column - half * len(near_refs)
    step = FAR[0] + lax.rem(far_column // rows, len(FAR))
    within = far_column // (rows * len(FAR)) * rows + lax.rem(column, rows)
    for number, behind in enumerate((0, *RING)):
        inside = column // half == number
        step = jnp.where(inside, behind, step)
        within = jnp.where(inside, column - number * half, within)
    block = lax.rem(ctx - step + blocks, blocks)
    k_pos = block * count + block_offset(within // rows, lax.rem(within, rows), core, rows)
    causal = q_pos >= k_pos

    compressed = split(latent[:, :rank], 2)
    key_up = jnp.concatenate([key_ref[...], far_key_ref[...]], axis=1)
    value_up = jnp.concatenate([value_ref[...], far_value_ref[...]], axis=1)
    keys = three(compressed, split(key_up, 2), nn)
    values = three(compressed, split(value_up, 2), nn)
    high, middle, low = split(latent[:, rank:], 3)
    shared_keys = [high, middle, low, high, middle, high]
    for head in range(heads):
        high, low = split(keys[:, head * nope : (head + 1) * nope], 2)
        key = jnp.concatenate([high, low, high, *shared_keys], axis=1)
        query = jnp.concatenate([mine_ref[head], theirs_ref[heads - 1 - head]], axis=0)
        query = query * (scale * LOG2E)
        high, low = split(query[:, :nope], 2)
        own_queries = [low, high, high]
        high, middle, low = split(query[:, nope:], 3)
        shared_queries = [low, middle, high, middle, high, high]
        scores = nt(jnp.concatenate(own_queries + shared_queries, axis=1), key)
        scores = jnp.where(causal, scores, FLOOR)
        top = jnp.max(scores, axis=1, keepdims=True)
        weight = jnp.exp2(scores - top)
        total = jnp.sum(weight, axis=1, keepdims=True)
        value = split(values[:, head * vdim : (head + 1) * vdim], 2)
        acc = three(split(weight, 2), value, nn)
        for number, out_ref in enumerate(out_refs):
            chosen = slice(number * half, (number + 1) * half)
            out_ref[head, :, :vdim] = acc[chosen]
            out_ref[head, :, vdim : vdim + 64] = jnp.broadcast_to(top[chosen], (half, 64))
            out_ref[head, :, vdim + 64 :] = jnp.broadcast_to(total[chosen], (half, 64))


def share_kernel(state_ref, arrived_ref, out_w_ref, out_ref):
    heads = state_ref.shape[0]
    vdim = out_w_ref.shape[1] // heads
    attended = []
    for head in range(heads):
        mine = state_ref[head]
        other = arrived_ref[heads - 1 - head]
        m0, m1 = mine[:, vdim : vdim + 1], other[:, vdim : vdim + 1]
        top = jnp.maximum(m0, m1)
        f0, f1 = jnp.exp2(m0 - top), jnp.exp2(m1 - top)
        total = mine[:, vdim + 64 : vdim + 65] * f0 + other[:, vdim + 64 : vdim + 65] * f1
        attended.append((mine[:, :vdim] * f0 + other[:, :vdim] * f1) / total)
    left = split(jnp.concatenate(attended, axis=1), 2)
    out_ref[...] = three(left, [out_w_ref[part] for part in range(2)], nn)


def partner(array):
    size = lax.axis_size("head")
    return lax.ppermute(array, "head", [(h, h ^ 1) for h in range(size)])


def from_behind(array, step):
    size = lax.axis_size("ctx")
    return lax.ppermute(array, "ctx", [(c, (c + step) % size) for c in range(size)])


def exchange(pieces):
    size = lax.axis_size("head")
    groups = [list(range(core, size, 2)) for core in range(2)]
    return lax.all_to_all(
        pieces, "head", split_axis=0, concat_axis=0, tiled=True, axis_index_groups=groups
    )


def spread_kernel(*refs):
    out_ref = refs[-1]
    for number, ref in enumerate(refs[:-1]):
        for copy in range(out_ref.shape[0]):
            out_ref[copy, number] = ref[...]


def on_device(hidden, w_query, w_down, latent_gain, w_key_up, w_value_up, w_out):
    rows, depth = hidden.shape
    blocks = lax.axis_size("ctx")
    places = lax.axis_size("head") // 2
    half = places * rows
    vdim = w_value_up.shape[1]
    width = w_down.shape[1]
    place = jnp.stack([lax.axis_index("ctx"), lax.axis_index("head") & 1]).astype(jnp.int32)
    gain = latent_gain[None]

    copies = call(spread_kernel, shape(places, 1, rows, depth), [hidden], "copies")
    mine = exchange(copies).reshape(half, depth)
    far_query, far_key, far_value, far_out = (
        partner(weight) for weight in (w_query, w_key_up, w_value_up, w_out)
    )
    own = call(own_kernel, shape(rows, width), [hidden, w_down.T, gain], "own_latent")
    far = [from_behind(own, step) for step in FAR]
    far, far_out = lax.optimization_barrier((far, far_out))
    far_copies = call(spread_kernel, shape(places, len(FAR), rows, width), far, "far_copies")
    far_latent = exchange(far_copies).reshape(-1, width)

    latent = call(latent_kernel, shape(half, width), [mine, w_down.T, gain], "latent")
    ring = [from_behind(latent, step) for step in RING]

    mine, far_query, _ = lax.optimization_barrier((mine, far_query, latent))
    queries = call(
        query_kernel,
        shape(2, half, w_query.shape[1]),
        [mine, w_query.T, far_query.T],
        "query",
    )
    other_queries = partner(queries)
    out_parts = call(
        functools.partial(split_kernel, 2),
        shape(2, 2 * vdim, depth, dtype=BF16),
        [w_out, far_out],
        "out_parts",
    )

    latent, out_parts = lax.optimization_barrier((latent, out_parts))
    state = call(
        functools.partial(attend_kernel, rows, w_query.shape[1] ** (-0.5), blocks),
        [shape(2, half, 2 * vdim)] * 2,
        [
            queries,
            other_queries,
            w_key_up,
            far_key,
            w_value_up,
            far_value,
            latent,
            *ring,
            far_latent,
        ],
        "attend",
        place,
    )
    arrived = partner(state[1])
    shares = call(share_kernel, shape(half, depth), [state[0], arrived, out_parts], "share")
    return exchange(shares.reshape(places, rows, depth)).sum(axis=0)


def solution(mesh):
    placed = (
        P(("ctx", "head"), None),
        P(None, "head"),
        P(),
        P(),
        P(None, "head"),
        P(None, "head"),
        P("head", None),
    )
    return jax.shard_map(
        on_device, mesh=mesh, in_specs=placed, out_specs=P(("ctx", "head"), None), check_vma=False
    )
```

```python
import functools

import jax
import jax.numpy as jnp
from jax import lax
from jax.experimental import pallas as pl
from jax.experimental.pallas import tpu as pltpu
from jax.sharding import PartitionSpec as P

EPSILON = 1e-06
FLOOR = -1e30
LOG2E = 1.4426950408889634
RING = (1, -1)
FAR = (2, 3, 4, 5, 6)
F32 = jnp.float32
BF16 = jnp.bfloat16
VMEM = pltpu.VMEM
LIMIT = 24 << 20


def nn(left, right):
    return lax.dot_general(left, right, (((1,), (0,)), ((), ())), preferred_element_type=F32)


def nt(left, right):
    return lax.dot_general(left, right, (((1,), (1,)), ((), ())), preferred_element_type=F32)


def split(array, count):
    parts = []
    for _ in range(count - 1):
        part = array.astype(BF16)
        parts.append(part)
        array = array - part.astype(F32)
    parts.append(array.astype(BF16))
    return parts


def six(left, right, dot):
    high, middle, low = left
    rows = high.shape[0]
    by_high = dot(jnp.concatenate([high, middle, low], axis=0), right[0])
    by_middle = dot(jnp.concatenate([high, middle], axis=0), right[1])
    by_low = dot(high, right[2])
    return by_high[:rows] + (
        (by_high[rows : 2 * rows] + by_middle[:rows])
        + (by_high[2 * rows :] + by_middle[rows:] + by_low)
    )


def three(left, right, dot):
    return dot(left[1], right[0]) + dot(left[0], right[1]) + dot(left[0], right[0])


def call(kernel, outs, operands, name, place=None):
    first = [] if place is None else [place]
    return pl.pallas_call(
        kernel,
        out_shape=outs,
        in_specs=[pl.BlockSpec(memory_space=pltpu.SMEM)] * len(first)
        + [pl.BlockSpec(memory_space=VMEM)] * len(operands),
        out_specs=jax.tree.map(lambda _: pl.BlockSpec(memory_space=VMEM), outs),
        compiler_params=pltpu.CompilerParams(vmem_limit_bytes=LIMIT),
        name=name,
    )(*first, *operands)


def shape(*dims, dtype=F32):
    return jax.ShapeDtypeStruct(dims, dtype)


def split_kernel(count, *refs):
    sources, outs = refs[:-1], refs[-1]
    start = 0
    for ref in sources:
        stop = start + ref.shape[0]
        for part, value in enumerate(split(ref[...], count)):
            outs[part, start:stop] = value
        start = stop


def normed(down, gain, out_ref):
    rank = gain.shape[1]
    raw = down[:, :rank]
    meansq = jnp.mean(raw * raw, axis=-1, keepdims=True)
    out_ref[:, :rank] = raw * lax.rsqrt(meansq + EPSILON) * gain
    out_ref[:, rank:] = down[:, rank:]


def own_kernel(x_ref, down_ref, gain_ref, out_ref):
    rows = x_ref.shape[0]
    x = jnp.concatenate([part.astype(F32) for part in split(x_ref[...], 3)], axis=0).astype(BF16)
    rank = gain_ref.shape[1]
    high, low = (nt(part, x) for part in split(down_ref[:rank], 2))
    raw = high[:, :rows] + (high[:, rows : 2 * rows] + low[:, :rows])
    high, middle, low = (nt(part, x) for part in split(down_ref[rank:], 3))
    shared = high[:, :rows] + (
        (high[:, rows : 2 * rows] + middle[:, :rows])
        + (high[:, 2 * rows :] + middle[:, rows : 2 * rows] + low[:, :rows])
    )
    normed(jnp.concatenate([raw, shared], axis=0).T, gain_ref[...], out_ref)


def latent_kernel(x_ref, down_ref, gain_ref, out_ref):
    rank = gain_ref.shape[1]
    x = split(x_ref[...], 3)
    rows = x_ref.shape[0]
    high, low = split(down_ref[:rank], 2)
    by_high = nt(jnp.concatenate(x[:2], axis=0), high)
    raw = by_high[:rows] + (by_high[rows:] + nt(x[0], low))
    shared = six(x, split(down_ref[rank:], 3), nt)
    normed(jnp.concatenate([raw, shared], axis=1), gain_ref[...], out_ref)


def query_kernel(x_ref, own_ref, other_ref, out_ref):
    x = split(x_ref[...], 3)
    out_ref[0] = six(x, split(own_ref[...], 3), nt)
    out_ref[1] = six(x, split(other_ref[...], 3), nt)


def block_offset(place, row, cls, rows):
    return (place * 2 + cls) * rows + row


def attend_kernel(rows, scale, blocks, place_ref, *refs):
    mine_ref, theirs_ref, key_ref, far_key_ref, value_ref, far_value_ref = refs[:6]
    near_refs, far_ref = refs[6:-3], refs[-3]
    out_refs = refs[-2:]
    ctx, core = place_ref[0], place_ref[1]
    rank, nope = key_ref.shape
    vdim = value_ref.shape[1]
    heads, half, _ = mine_ref.shape
    count = 2 * half

    row = lax.broadcasted_iota(jnp.int32, (count, 1), 0)
    row_cls = jnp.where(row < half, core, 1 - core)
    within = lax.rem(row, half)
    q_pos = ctx * count + block_offset(within // rows, lax.rem(within, rows), row_cls, rows)

    latent = jnp.concatenate([ref[...] for ref in near_refs] + [far_ref[...]], axis=0)
    column = lax.broadcasted_iota(jnp.int32, (1, latent.shape[0]), 1)
    far_column = column - half * len(near_refs)
    step = FAR[0] + lax.rem(far_column // rows, len(FAR))
    within = far_column // (rows * len(FAR)) * rows + lax.rem(column, rows)
    for number, behind in enumerate((0, *RING)):
        inside = column // half == number
        step = jnp.where(inside, behind, step)
        within = jnp.where(inside, column - number * half, within)
    block = lax.rem(ctx - step + blocks, blocks)
    k_pos = block * count + block_offset(within // rows, lax.rem(within, rows), core, rows)
    causal = q_pos >= k_pos

    compressed = split(latent[:, :rank], 2)
    key_up = jnp.concatenate([key_ref[...], far_key_ref[...]], axis=1)
    value_up = jnp.concatenate([value_ref[...], far_value_ref[...]], axis=1)
    keys = three(compressed, split(key_up, 2), nn)
    values = three(compressed, split(value_up, 2), nn)
    high, middle, low = split(latent[:, rank:], 3)
    shared_keys = [high, middle, low, high, middle, high]
    for head in range(heads):
        high, low = split(keys[:, head * nope : (head + 1) * nope], 2)
        key = jnp.concatenate([high, low, high, *shared_keys], axis=1)
        query = jnp.concatenate([mine_ref[head], theirs_ref[heads - 1 - head]], axis=0)
        query = query * (scale * LOG2E)
        high, low = split(query[:, :nope], 2)
        own_queries = [low, high, high]
        high, middle, low = split(query[:, nope:], 3)
        shared_queries = [low, middle, high, middle, high, high]
        scores = nt(jnp.concatenate(own_queries + shared_queries, axis=1), key)
        scores = jnp.where(causal, scores, FLOOR)
        top = jnp.max(scores, axis=1, keepdims=True)
        weight = jnp.exp2(scores - top)
        total = jnp.sum(weight, axis=1, keepdims=True)
        value = split(values[:, head * vdim : (head + 1) * vdim], 2)
        acc = three(split(weight, 2), value, nn)
        for number, out_ref in enumerate(out_refs):
            chosen = slice(number * half, (number + 1) * half)
            out_ref[head, :, :vdim] = acc[chosen]
            out_ref[head, :, vdim : vdim + 64] = jnp.broadcast_to(top[chosen], (half, 64))
            out_ref[head, :, vdim + 64 :] = jnp.broadcast_to(total[chosen], (half, 64))


def share_kernel(state_ref, arrived_ref, out_w_ref, out_ref):
    heads = state_ref.shape[0]
    vdim = out_w_ref.shape[1] // heads
    attended = []
    for head in range(heads):
        mine = state_ref[head]
        other = arrived_ref[heads - 1 - head]
        m0, m1 = mine[:, vdim : vdim + 1], other[:, vdim : vdim + 1]
        top = jnp.maximum(m0, m1)
        f0, f1 = jnp.exp2(m0 - top), jnp.exp2(m1 - top)
        total = mine[:, vdim + 64 : vdim + 65] * f0 + other[:, vdim + 64 : vdim + 65] * f1
        attended.append((mine[:, :vdim] * f0 + other[:, :vdim] * f1) / total)
    left = split(jnp.concatenate(attended, axis=1), 2)
    out_ref[...] = three(left, [out_w_ref[part] for part in range(2)], nn)


def partner(array):
    size = lax.axis_size("head")
    return lax.ppermute(array, "head", [(h, h ^ 1) for h in range(size)])


def from_behind(array, step):
    size = lax.axis_size("ctx")
    return lax.ppermute(array, "ctx", [(c, (c + step) % size) for c in range(size)])


def exchange(pieces):
    size = lax.axis_size("head")
    groups = [list(range(core, size, 2)) for core in range(2)]
    return lax.all_to_all(
        pieces, "head", split_axis=0, concat_axis=0, tiled=True, axis_index_groups=groups
    )


def spread_kernel(*refs):
    out_ref = refs[-1]
    for number, ref in enumerate(refs[:-1]):
        for copy in range(out_ref.shape[0]):
            out_ref[copy, number] = ref[...]


def on_device(hidden, w_query, w_down, latent_gain, w_key_up, w_value_up, w_out):
    rows, depth = hidden.shape
    blocks = lax.axis_size("ctx")
    places = lax.axis_size("head") // 2
    half = places * rows
    vdim = w_value_up.shape[1]
    width = w_down.shape[1]
    place = jnp.stack([lax.axis_index("ctx"), lax.axis_index("head") & 1]).astype(jnp.int32)
    gain = latent_gain[None]

    copies = call(spread_kernel, shape(places, 1, rows, depth), [hidden], "copies")
    mine = exchange(copies).reshape(half, depth)
    far_query, far_key, far_value, far_out = (
        partner(weight) for weight in (w_query, w_key_up, w_value_up, w_out)
    )
    own = call(own_kernel, shape(rows, width), [hidden, w_down.T, gain], "own_latent")
    far = [from_behind(own, step) for step in FAR]
    far, far_out = lax.optimization_barrier((far, far_out))
    far_copies = call(spread_kernel, shape(places, len(FAR), rows, width), far, "far_copies")
    far_latent = exchange(far_copies).reshape(-1, width)

    latent = call(latent_kernel, shape(half, width), [mine, w_down.T, gain], "latent")
    ring = [from_behind(latent, 1), lax.ppermute(latent, "ctx", [(0, blocks - 1)])]

    mine, far_query, _ = lax.optimization_barrier((mine, far_query, latent))
    queries = call(
        query_kernel,
        shape(2, half, w_query.shape[1]),
        [mine, w_query.T, far_query.T],
        "query",
    )
    other_queries = partner(queries)
    out_parts = call(
        functools.partial(split_kernel, 2),
        shape(2, 2 * vdim, depth, dtype=BF16),
        [w_out, far_out],
        "out_parts",
    )

    latent, out_parts = lax.optimization_barrier((latent, out_parts))
    state = call(
        functools.partial(attend_kernel, rows, w_query.shape[1] ** (-0.5), blocks),
        [shape(2, half, 2 * vdim)] * 2,
        [
            queries,
            other_queries,
            w_key_up,
            far_key,
            w_value_up,
            far_value,
            latent,
            *ring,
            far_latent,
        ],
        "attend",
        place,
    )
    arrived = partner(state[1])
    shares = call(share_kernel, shape(half, depth), [state[0], arrived, out_parts], "share")
    return exchange(shares.reshape(places, rows, depth)).sum(axis=0)


def solution(mesh):
    placed = (
        P(("ctx", "head"), None),
        P(None, "head"),
        P(),
        P(),
        P(None, "head"),
        P(None, "head"),
        P("head", None),
    )
    return jax.shard_map(
        on_device, mesh=mesh, in_specs=placed, out_specs=P(("ctx", "head"), None), check_vma=False
    )
```
